512 devices in a mesh: state: 4 (over y), aux: 32 (over z, x_hi), cond: 4 (over x_lo, core).
Axes of the slice: x: 4 (x_hi: 2, x_lo: 2; x = x_hi * 2 + x_lo), y: 4, z: 16, core: 2. Of those that a mesh axis runs over, the one named last changes fastest.
Arguments:
- cond_pairs: float32 [128, 1024, 1024], P('aux', 'cond', 'state'), may hold values from -0.1875 to 0.1875
- val_pairs: float32 [128, 512, 512], P('aux', 'state', 'cond'), may hold values from -0.25 to 0.25
- screened: float32 [128, 128], replicated, may hold values from -0.046875 to 0.046875
- trials: float32 [8, 1024, 512], P('state', 'cond'), may hold values from -6 to 6
Outputs:
- response: float32 [8, 1024, 512], P('state', 'cond')
The draws below stay inside these ranges and needn't reach their ends.
All inputs are finite; a program needn't handle non-finite values.
Results may differ from the reference program's by a relative error of at most 0.0001.
Values sent between devices are 32-bit elements; how exact they have to be, the bound alone decides.
No kernel may reach another device: no remote copies, remote signals or barrier semaphores. Data moves between devices by JAX's collectives and lax.ppermute only.
A program may use at most 64 MiB of HBM per device.

```python
import jax
import jax.numpy as jnp
from jax import lax

NC = 1024
NV = 512
NT = 8
NAUX = 128


def block_scale(rng, extent, pieces, least, top_value):
    gain = 1.0
    for dim, shards_of in pieces:
        draws = jax.random.uniform(jax.random.fold_in(jax.random.fold_in(rng, 6), dim), (shards_of,), jnp.float32, least / len(pieces), top_value / len(pieces))
        gain = gain * jnp.repeat(jnp.exp(draws), extent[dim] // shards_of).reshape((-1,) + (1,) * (len(extent) - 1 - dim))
    return gain


def gaussian(key, shape, deviation, reach, shards=(), dtype=jnp.bfloat16):
    values = jax.random.normal(key, shape, jnp.float32) * deviation
    if len(shards) > 0:
        values = block_scale(key, shape, shards, -0.22, 0.18) * values
    return jnp.clip(values, min=-reach, max=reach).astype(dtype)


def setup_inputs(seed: int = 0) -> dict:
    keys = jax.random.split(jax.random.key(seed), 5)
    return {
        "cond_pairs": gaussian(keys[0], (NAUX, NC, NC), NC ** -0.5, 0.1875, ((0, 32), (1, 4), (2, 4)), jnp.float32),
        "val_pairs": gaussian(keys[1], (NAUX, NV, NV), NV ** -0.5, 0.25, ((0, 32), (1, 4), (2, 4)), jnp.float32),
        "screened": gaussian(keys[2], (NAUX, NAUX), (NAUX * NAUX) ** -0.5, 0.046875, (), jnp.float32),
        "trials": gaussian(keys[3], (NT, NC, NV), 1.0, 6.0, ((0, 4), (1, 4)), jnp.float32),
    }


highest = lax.Precision.HIGHEST


def reference(cond_pairs, val_pairs, screened, trials):
    coupled = jnp.einsum("pq,qab->pab", screened, val_pairs, precision=highest)

    def add_aux(running, scanned):
        slab_block, pair_block = scanned
        mixture = jnp.einsum("cd,ndv->ncv", slab_block, trials, precision=highest)
        return running + jnp.einsum("ncv,vw->ncw", mixture, pair_block, precision=highest), None

    start_value = jnp.zeros(trials.shape, jnp.float32)
    response, unused = lax.scan(add_aux, start_value, (cond_pairs, coupled))
    return response
```

```python
import jax
import jax.numpy as jnp
from jax import lax
from jax.experimental import pallas as pl
from jax.experimental.pallas import tpu as pltpu
from jax.sharding import PartitionSpec as P


AXES = ("state", "aux", "cond")
SHIFTS = (0, 1, -1, 2)
highest = lax.Precision.HIGHEST
f32, bf16 = jnp.float32, jnp.bfloat16


def split(value):
    upper = value.astype(bf16)
    return upper, (value - upper.astype(f32)).astype(bf16)


def dot3(a, b):
    (ah, al), (bh, bl) = a, b
    dot = lambda x, y: jnp.dot(x, y, preferred_element_type=f32)
    return dot(ah, bh) + (dot(ah, bl) + dot(al, bh))


def mix_kernel(*refs):
    slabs, pieces, (mh, ml), (b_all, x_all, bh, bl, xh, xl, sems) = refs[:4], refs[4:8], refs[8:10], refs[10:]
    n_p, _, width = slabs[0].shape
    n_n = pieces[0].shape[0]
    s, k = lax.axis_index("state"), lax.axis_index("cond")
    copies = []
    for i, shift in enumerate(SHIFTS):
        start = pl.multiple_of(lax.rem(s + 4 - shift, 4) * width, width)
        copies.append(pltpu.make_async_copy(slabs[i], b_all.at[:, :, pl.ds(start, width)], sems.at[i]))
    for i in range(4):
        copies.append(pltpu.make_async_copy(pieces[i], x_all.at[jnp.bitwise_xor(k, i)], sems.at[4 + i]))
    for copy in copies:
        copy.start()
    for copy in copies[4:]:
        copy.wait()

    @pl.loop(0, 4)
    def _(j):
        for n in range(n_n):
            at = pl.ds(pl.multiple_of(j * width, width), width)
            xh[n, at, :], xl[n, at, :] = split(x_all[j, n])

    for copy in copies[:4]:
        copy.wait()

    @pl.loop(0, n_p)
    def _(p):
        bh[...], bl[...] = split(b_all[p])

        @pl.loop(0, n_n)
        def _(n):
            mh[n, p], ml[n, p] = split(dot3((bh[...], bl[...]), (xh[n], xl[n])))


def mix(slabs, pieces):
    n_p, rows, width = slabs[0].shape
    n_n, _, cols = pieces[0].shape
    any_spec = pl.BlockSpec(memory_space=pl.ANY)
    vmem = pl.BlockSpec(memory_space=pltpu.VMEM)
    shape = jax.ShapeDtypeStruct((n_n, n_p, rows, cols), bf16)
    return pl.pallas_call(
        mix_kernel,
        name="mix",
        out_shape=(shape, shape),
        in_specs=[any_spec] * 8,
        out_specs=(vmem, vmem),
        scratch_shapes=[
            pltpu.VMEM((n_p, rows, 4 * width), f32),
            pltpu.VMEM((4, n_n, width, cols), f32),
            pltpu.VMEM((rows, 4 * width), bf16),
            pltpu.VMEM((rows, 4 * width), bf16),
            pltpu.VMEM((n_n, 4 * width, cols), bf16),
            pltpu.VMEM((n_n, 4 * width, cols), bf16),
            pltpu.SemaphoreType.DMA((8,)),
        ],
        cost_estimate=pl.CostEstimate(flops=3 * 2 * n_n * n_p * rows * 4 * width * cols, transcendentals=0, bytes_accessed=1 << 24),
    )(*slabs, *pieces)


def product_into(out, m_pair, c_pair, n):
    mh, ml = m_pair
    ch, cl = c_pair
    out[...] = jnp.zeros_like(out)

    @pl.loop(0, mh.shape[1])
    def _(p):
        out[...] += dot3((mh[n, p], ml[n, p]), (ch[p], cl[p]))


def theirs_kernel(*refs):
    mh, ml, bands, mates, (out, ch, cl), (c_all, sems) = refs[0], refs[1], refs[2:6], refs[6:10], refs[10:13], refs[13:]
    n_x, n_p, v1, v2 = bands[0].shape
    s, half, core = lax.axis_index("state"), lax.rem(lax.axis_index("aux"), 2), lax.rem(lax.axis_index("cond"), 2)
    copies = []
    for i, shift in enumerate(SHIFTS):
        row = pl.multiple_of(lax.rem(s + 4 - shift, 4) * v1, v1)
        for x in range(n_x):
            for band, at in ((bands[i], core), (mates[i], 1 - core)):
                col = pl.multiple_of((2 * x + at) * v2, v2)
                target = c_all.at[:, pl.ds(row, v1), pl.ds(col, v2)]
                copies.append(pltpu.make_async_copy(band.at[x], target, sems.at[len(copies)]))
    for copy in copies:
        copy.start()
    for copy in copies:
        copy.wait()

    @pl.loop(0, n_p)
    def _(p):
        ch[p], cl[p] = split(c_all[p])

    product_into(out, (mh, ml), (ch, cl), 1 - half)


def mine_kernel(mh, ml, ch, cl, out):
    product_into(out, (mh, ml), (ch, cl), lax.rem(lax.axis_index("aux"), 2))


def respond(m_pair, bands, mates):
    _, n_p, rows, cols = m_pair[0].shape
    any_spec = pl.BlockSpec(memory_space=pl.ANY)
    vmem = pl.BlockSpec(memory_space=pltpu.VMEM)
    part = jax.ShapeDtypeStruct((rows, cols), f32)
    full = jax.ShapeDtypeStruct((n_p, cols, cols), bf16)
    cost = pl.CostEstimate(flops=3 * 2 * n_p * rows * cols * cols, transcendentals=0, bytes_accessed=1 << 23)
    theirs, ch, cl = pl.pallas_call(
        theirs_kernel,
        name="theirs",
        out_shape=(part, full, full),
        in_specs=[vmem] * 2 + [any_spec] * 8,
        out_specs=(vmem,) * 3,
        scratch_shapes=[pltpu.VMEM((n_p, cols, cols), f32), pltpu.SemaphoreType.DMA((16,))],
        cost_estimate=cost,
    )(*m_pair, *bands, *mates)
    mine = pl.pallas_call(
        mine_kernel, name="mine", out_shape=part, in_specs=[vmem] * 4, out_specs=vmem, cost_estimate=cost
    )(*m_pair, ch, cl)
    return theirs, mine


def moves(mesh, step):
    n_state, n_aux, n_cond = (mesh.shape[name] for name in AXES)

    def number(y, z, x, core):
        n_z = n_aux // 2
        y, z, x, core = y % n_state, z % n_z, x % 4, core % 2
        return (y * n_aux + z * 2 + x // 2) * n_cond + (x % 2) * 2 + core

    places = [
        (y, z, x, core)
        for y in range(n_state)
        for z in range(n_aux // 2)
        for x in range(4)
        for core in range(2)
    ]
    return [(number(*place), number(*step(*place))) for place in places]


def solution(mesh):
    to_core = moves(mesh, lambda y, z, x, c: (y, z, x, 1 - c))
    to_x = {d: moves(mesh, lambda y, z, x, c, d=d: (y, z, x + d, c)) for d in (1, -1, 2)}
    to_pair = moves(mesh, lambda y, z, x, c: (y, z, x ^ 1, c))
    to_y = {d: moves(mesh, lambda y, z, x, c, d=d: (y + d, z, x, c)) for d in (1, -1, 2)}
    n_z = mesh.shape["aux"] // 2
    along_z = [[2 * z + half for z in range(n_z)] for half in range(2)]

    def send(value, pairs):
        return lax.ppermute(value, AXES, pairs)

    def per_device(cond_pairs, val_pairs, screened, trials):
        n_p, rows, _ = cond_pairs.shape
        half = lax.axis_index("aux") % 2
        x_lo = lax.axis_index("cond") // 2

        slabs = [cond_pairs]
        for d in SHIFTS[1:]:
            slabs.append(send(cond_pairs, to_y[d]))
        far = jnp.stack([send(trials[0], to_x[1]), send(trials[1], to_x[-1])])
        pieces = [trials, send(trials, to_core), far, send(far, to_core)]

        qb, v1, v2 = val_pairs.shape
        spread = val_pairs.reshape(qb, n_z, v1 // n_z, v2).transpose(1, 0, 2, 3)
        spread = lax.all_to_all(spread, "aux", 0, 0, axis_index_groups=along_z)
        w = screened.reshape(n_z, 2, n_p, n_z, 2, qb)
        w = lax.dynamic_index_in_dim(w, half, 4, keepdims=False)
        w_own = lax.dynamic_index_in_dim(w, half, 1, keepdims=False)
        w_other = lax.dynamic_index_in_dim(w, 1 - half, 1, keepdims=False)
        product = lambda m: jnp.einsum("apzq,zqrv->aprv", m, spread, precision=highest)
        swapped = send(product(w_other), to_x[2])
        block = product(w_own) + swapped
        block = lax.all_to_all(block, "aux", 0, 0, axis_index_groups=along_z)
        block = block.transpose(1, 0, 2, 3).reshape(n_p, v1, v2)

        other = send(block, to_pair)
        two = jnp.stack([jnp.where(x_lo == 0, block, other), jnp.where(x_lo == 0, other, block)])
        bands = [two]
        for d in SHIFTS[1:]:
            bands.append(send(two, to_y[d]))
        mates = [send(band, to_core) for band in bands]

        theirs, mine = respond(mix(slabs, pieces), bands, mates)

        mine = mine + send(theirs, to_x[2])
        parts = mine.reshape(n_z, rows // n_z, mine.shape[1])
        parts = lax.all_to_all(parts, "aux", 0, 0, axis_index_groups=along_z)
        total = jnp.sum(parts, axis=0)
        total = lax.all_gather(total, "aux", axis=0, tiled=True, axis_index_groups=along_z)
        opposite = send(total, to_x[2])
        return jnp.stack([jnp.where(half == 0, total, opposite), jnp.where(half == 0, opposite, total)])

    in_specs = (P("aux", "cond", "state"), P("aux", "state", "cond"), P(), P("state", "cond", None))
    return jax.shard_map(per_device, mesh=mesh, in_specs=in_specs, out_specs=P("state", "cond", None), check_vma=False)
```

```python
import jax
import jax.numpy as jnp
from jax import lax
from jax.experimental import pallas as pl
from jax.experimental.pallas import tpu as pltpu
from jax.sharding import PartitionSpec as P


AXES = ("state", "aux", "cond")
SHIFTS = (0, 1, -1, 2)
highest = lax.Precision.HIGHEST
f32, bf16 = jnp.float32, jnp.bfloat16


def split(value):
    upper = value.astype(bf16)
    return upper, (value - upper.astype(f32)).astype(bf16)


def dot3(a, b):
    (ah, al), (bh, bl) = a, b
    dot = lambda x, y: jnp.dot(x, y, preferred_element_type=f32)
    return dot(ah, bh) + (dot(ah, bl) + dot(al, bh))


def mix_kernel(*refs):
    slabs, pieces, (mh, ml), (b_all, x_all, bh, bl, xh, xl, sems) = refs[:4], refs[4:8], refs[8:10], refs[10:]
    n_p, _, width = slabs[0].shape
    n_n = pieces[0].shape[0]
    s, k = lax.axis_index("state"), lax.axis_index("cond")
    copies = []
    for i, shift in enumerate(SHIFTS):
        start = pl.multiple_of(lax.rem(s + 4 - shift, 4) * width, width)
        copies.append(pltpu.make_async_copy(slabs[i], b_all.at[:, :, pl.ds(start, width)], sems.at[i]))
    for i in range(4):
        copies.append(pltpu.make_async_copy(pieces[i], x_all.at[jnp.bitwise_xor(k, i)], sems.at[4 + i]))
    for copy in copies:
        copy.start()
    for copy in copies[4:]:
        copy.wait()

    @pl.loop(0, 4)
    def _(j):
        for n in range(n_n):
            at = pl.ds(pl.multiple_of(j * width, width), width)
            xh[n, at, :], xl[n, at, :] = split(x_all[j, n])

    for copy in copies[:4]:
        copy.wait()

    @pl.loop(0, n_p)
    def _(p):
        bh[...], bl[...] = split(b_all[p])

        @pl.loop(0, n_n)
        def _(n):
            mh[n, p], ml[n, p] = split(dot3((bh[...], bl[...]), (xh[n], xl[n])))


def mix(slabs, pieces):
    n_p, rows, width = slabs[0].shape
    n_n, _, cols = pieces[0].shape
    any_spec = pl.BlockSpec(memory_space=pl.ANY)
    vmem = pl.BlockSpec(memory_space=pltpu.VMEM)
    shape = jax.ShapeDtypeStruct((n_n, n_p, rows, cols), bf16)
    return pl.pallas_call(
        mix_kernel,
        name="mix",
        out_shape=(shape, shape),
        in_specs=[any_spec] * 8,
        out_specs=(vmem, vmem),
        scratch_shapes=[
            pltpu.VMEM((n_p, rows, 4 * width), f32),
            pltpu.VMEM((4, n_n, width, cols), f32),
            pltpu.VMEM((rows, 4 * width), bf16),
            pltpu.VMEM((rows, 4 * width), bf16),
            pltpu.VMEM((n_n, 4 * width, cols), bf16),
            pltpu.VMEM((n_n, 4 * width, cols), bf16),
            pltpu.SemaphoreType.DMA((8,)),
        ],
        compiler_params=pltpu.CompilerParams(vmem_limit_bytes=28 << 20),
        cost_estimate=pl.CostEstimate(
            flops=3 * 2 * n_n * n_p * rows * 4 * width * cols, transcendentals=0, bytes_accessed=1 << 24
        ),
    )(*slabs, *pieces)


def respond_kernel(*refs):
    mh, ml, bands, mates, (out, c_all, ch, cl, sems) = refs[0], refs[1], refs[2:6], refs[6:10], refs[10:]
    n_x, n_p, v1, v2 = bands[0].shape
    s, core = lax.axis_index("state"), lax.rem(lax.axis_index("cond"), 2)
    copies = []
    for i, shift in enumerate(SHIFTS):
        row = pl.multiple_of(lax.rem(s + 4 - shift, 4) * v1, v1)
        for x in range(n_x):
            for band, at in ((bands[i], core), (mates[i], 1 - core)):
                col = pl.multiple_of((2 * x + at) * v2, v2)
                target = c_all.at[:, pl.ds(row, v1), pl.ds(col, v2)]
                copies.append(pltpu.make_async_copy(band.at[x], target, sems.at[len(copies)]))
    for copy in copies:
        copy.start()
    out[...] = jnp.zeros_like(out)
    for copy in copies:
        copy.wait()

    @pl.loop(0, n_p)
    def _(p):
        ch[...], cl[...] = split(c_all[p])

        @pl.loop(0, out.shape[0])
        def _(n):
            out[n] += dot3((mh[n, p], ml[n, p]), (ch[...], cl[...]))


def respond(m_pair, bands, mates):
    n_n, n_p, rows, cols = m_pair[0].shape
    any_spec = pl.BlockSpec(memory_space=pl.ANY)
    vmem = pl.BlockSpec(memory_space=pltpu.VMEM)
    return pl.pallas_call(
        respond_kernel,
        name="respond",
        out_shape=jax.ShapeDtypeStruct((n_n, rows, cols), f32),
        in_specs=[vmem] * 2 + [any_spec] * 8,
        out_specs=vmem,
        scratch_shapes=[
            pltpu.VMEM((n_p, cols, cols), f32),
            pltpu.VMEM((cols, cols), bf16),
            pltpu.VMEM((cols, cols), bf16),
            pltpu.SemaphoreType.DMA((16,)),
        ],
        compiler_params=pltpu.CompilerParams(vmem_limit_bytes=28 << 20),
        cost_estimate=pl.CostEstimate(
            flops=3 * 2 * n_n * n_p * rows * cols * cols, transcendentals=0, bytes_accessed=1 << 24
        ),
    )(*m_pair, *bands, *mates)


def moves(mesh, step):
    n_state, n_aux, n_cond = (mesh.shape[name] for name in AXES)

    def number(y, z, x, core):
        n_z = n_aux // 2
        y, z, x, core = y % n_state, z % n_z, x % 4, core % 2
        return (y * n_aux + z * 2 + x // 2) * n_cond + (x % 2) * 2 + core

    places = [
        (y, z, x, core)
        for y in range(n_state)
        for z in range(n_aux // 2)
        for x in range(4)
        for core in range(2)
    ]
    return [(number(*place), number(*step(*place))) for place in places]


def solution(mesh):
    to_core = moves(mesh, lambda y, z, x, c: (y, z, x, 1 - c))
    to_x = moves(mesh, lambda y, z, x, c: (y, z, x + 2, c))
    to_pair = moves(mesh, lambda y, z, x, c: (y, z, x ^ 1, c))
    to_y = {d: moves(mesh, lambda y, z, x, c, d=d: (y + d, z, x, c)) for d in (1, -1, 2)}
    n_z = mesh.shape["aux"] // 2
    along_z = [[2 * z + half for z in range(n_z)] for half in range(2)]
    fours = [[4 * g + t for t in range(4)] for g in range(n_z // 2)]
    along_fours = [[4 * g + t for g in range(n_z // 2)] for t in range(4)]

    def send(value, pairs):
        return lax.ppermute(value, AXES, pairs)

    def per_device(cond_pairs, val_pairs, screened, trials):
        n_p, _, _ = cond_pairs.shape
        half = lax.axis_index("aux") % 2
        x_lo = lax.axis_index("cond") // 2

        slabs = [cond_pairs]
        for d in SHIFTS[1:]:
            slabs.append(send(cond_pairs, to_y[d]))
        far = send(trials, to_pair)
        pieces = [trials, send(trials, to_core), far]
        pieces.append(send(far, to_core))

        qb, v1, v2 = val_pairs.shape
        spread = val_pairs.reshape(qb, n_z, v1 // n_z, v2).transpose(1, 0, 2, 3)
        spread = lax.all_to_all(spread, "aux", 0, 0, axis_index_groups=along_z)
        n_q = screened.shape[0]
        q = lax.broadcasted_iota(jnp.int32, (n_q, n_q // 2), 0)
        j = lax.broadcasted_iota(jnp.int32, (n_q, n_q // 2), 1)
        picks = (q == (j // qb) * (2 * qb) + half * qb + j % qb).astype(f32)
        columns = jnp.dot(screened, picks, precision=highest)
        spread = spread.reshape(n_q // 2, v1 // n_z, v2)
        product = jnp.einsum("pq,qrv->prv", columns, spread, precision=highest)
        product = product.reshape(n_z, 2, n_p, v1 // n_z, v2)
        swapped = send(lax.dynamic_index_in_dim(product, 1 - half, 1, keepdims=False), to_x)
        block = lax.dynamic_index_in_dim(product, half, 1, keepdims=False) + swapped
        block = lax.all_to_all(block, "aux", 0, 0, axis_index_groups=along_z)
        block = block.transpose(1, 0, 2, 3).reshape(n_p, v1, v2)

        other = send(block, to_pair)
        two = jnp.stack([jnp.where(x_lo == 0, block, other), jnp.where(x_lo == 0, other, block)])
        bands = [two]
        for d in SHIFTS[1:]:
            bands.append(send(two, to_y[d]))
        mates = [send(band, to_core) for band in bands]

        m_pair = mix(slabs, pieces)
        partial = respond(m_pair, bands, mates)

        swap = lambda value, groups: lax.all_to_all(value, "aux", 0, 0, axis_index_groups=groups)
        parts = jnp.sum(swap(partial.reshape(4, -1, partial.shape[2]), fours), axis=0)
        parts = jnp.sum(swap(parts.reshape(n_z // 2, -1, parts.shape[1]), along_fours), axis=0)
        total = lax.all_gather(parts, "aux", axis=0, tiled=True, axis_index_groups=along_fours)
        total = swap(jnp.broadcast_to(total, (4, *total.shape)), fours)
        return total.reshape(partial.shape)

    in_specs = (P("aux", "cond", "state"), P("aux", "state", "cond"), P(), P("state", "cond", None))
    return jax.shard_map(per_device, mesh=mesh, in_specs=in_specs, out_specs=P("state", "cond", None), check_vma=False)
```

```python
import jax
import jax.numpy as jnp
from jax import lax
from jax.experimental import pallas as pl
from jax.experimental.pallas import tpu as pltpu
from jax.sharding import PartitionSpec as P


AXES = ("state", "aux", "cond")
SHIFTS = (0, 1, -1, 2)
highest = lax.Precision.HIGHEST
f32, bf16 = jnp.float32, jnp.bfloat16


def split(value):
    upper = value.astype(bf16)
    return upper, (value - upper.astype(f32)).astype(bf16)


def dot3(a, b):
    (ah, al), (bh, bl) = a, b
    dot = lambda x, y: jnp.dot(x, y, preferred_element_type=f32)
    return dot(ah, bh) + (dot(ah, bl) + dot(al, bh))


def mix_kernel(*refs):
    slabs, pieces, (mh, ml), (b_all, x_all, bh, bl, xh, xl, sems) = refs[:4], refs[4:8], refs[8:10], refs[10:]
    n_p, _, width = slabs[0].shape
    n_n = pieces[0].shape[0]
    s, k = lax.axis_index("state"), lax.axis_index("cond")
    copies = []
    for i, shift in enumerate(SHIFTS):
        start = pl.multiple_of(lax.rem(s + 4 - shift, 4) * width, width)
        copies.append(pltpu.make_async_copy(slabs[i], b_all.at[:, :, pl.ds(start, width)], sems.at[i]))
    for i in range(4):
        copies.append(pltpu.make_async_copy(pieces[i], x_all.at[jnp.bitwise_xor(k, i)], sems.at[4 + i]))
    for copy in copies:
        copy.start()
    for copy in copies[4:]:
        copy.wait()

    @pl.loop(0, 4)
    def _(j):
        for n in range(n_n):
            at = pl.ds(pl.multiple_of(j * width, width), width)
            xh[n, at, :], xl[n, at, :] = split(x_all[j, n])

    for copy in copies[:4]:
        copy.wait()

    @pl.loop(0, n_p)
    def _(p):
        bh[...], bl[...] = split(b_all[p])

        @pl.loop(0, n_n)
        def _(n):
            mh[n, p], ml[n, p] = split(dot3((bh[...], bl[...]), (xh[n], xl[n])))


def mix(slabs, pieces):
    n_p, rows, width = slabs[0].shape
    n_n, _, cols = pieces[0].shape
    any_spec = pl.BlockSpec(memory_space=pl.ANY)
    vmem = pl.BlockSpec(memory_space=pltpu.VMEM)
    shape = jax.ShapeDtypeStruct((n_n, n_p, rows, cols), bf16)
    return pl.pallas_call(
        mix_kernel,
        name="mix",
        out_shape=(shape, shape),
        in_specs=[any_spec] * 8,
        out_specs=(vmem, vmem),
        scratch_shapes=[
            pltpu.VMEM((n_p, rows, 4 * width), f32),
            pltpu.VMEM((4, n_n, width, cols), f32),
            pltpu.VMEM((rows, 4 * width), bf16),
            pltpu.VMEM((rows, 4 * width), bf16),
            pltpu.VMEM((n_n, 4 * width, cols), bf16),
            pltpu.VMEM((n_n, 4 * width, cols), bf16),
            pltpu.SemaphoreType.DMA((8,)),
        ],
        compiler_params=pltpu.CompilerParams(vmem_limit_bytes=28 << 20),
        cost_estimate=pl.CostEstimate(
            flops=3 * 2 * n_n * n_p * rows * 4 * width * cols, transcendentals=0, bytes_accessed=1 << 24
        ),
    )(*slabs, *pieces)


def respond_kernel(*refs):
    mh, ml, bands, mates, (out, c_all, ch, cl, sems) = refs[0], refs[1], refs[2:6], refs[6:10], refs[10:]
    n_x, n_p, v1, v2 = bands[0].shape
    s, core = lax.axis_index("state"), lax.rem(lax.axis_index("cond"), 2)
    copies = []
    for i, shift in enumerate(SHIFTS):
        row = pl.multiple_of(lax.rem(s + 4 - shift, 4) * v1, v1)
        for x in range(n_x):
            for band, at in ((bands[i], core), (mates[i], 1 - core)):
                col = pl.multiple_of((2 * x + at) * v2, v2)
                target = c_all.at[:, pl.ds(row, v1), pl.ds(col, v2)]
                copies.append(pltpu.make_async_copy(band.at[x], target, sems.at[len(copies)]))
    for copy in copies:
        copy.start()
    out[...] = jnp.zeros_like(out)
    for copy in copies:
        copy.wait()

    @pl.loop(0, n_p)
    def _(p):
        ch[...], cl[...] = split(c_all[p])

        @pl.loop(0, out.shape[0])
        def _(n):
            out[n] += dot3((mh[n, p], ml[n, p]), (ch[...], cl[...]))


def respond(m_pair, bands, mates):
    n_n, n_p, rows, cols = m_pair[0].shape
    any_spec = pl.BlockSpec(memory_space=pl.ANY)
    vmem = pl.BlockSpec(memory_space=pltpu.VMEM)
    return pl.pallas_call(
        respond_kernel,
        name="respond",
        out_shape=jax.ShapeDtypeStruct((n_n, rows, cols), f32),
        in_specs=[vmem] * 2 + [any_spec] * 8,
        out_specs=vmem,
        scratch_shapes=[
            pltpu.VMEM((n_p, cols, cols), f32),
            pltpu.VMEM((cols, cols), bf16),
            pltpu.VMEM((cols, cols), bf16),
            pltpu.SemaphoreType.DMA((16,)),
        ],
        compiler_params=pltpu.CompilerParams(vmem_limit_bytes=28 << 20),
        cost_estimate=pl.CostEstimate(
            flops=3 * 2 * n_n * n_p * rows * cols * cols, transcendentals=0, bytes_accessed=1 << 24
        ),
    )(*m_pair, *bands, *mates)


def moves(mesh, step):
    n_state, n_aux, n_cond = (mesh.shape[name] for name in AXES)

    def number(y, z, x, core):
        n_z = n_aux // 2
        y, z, x, core = y % n_state, z % n_z, x % 4, core % 2
        return (y * n_aux + z * 2 + x // 2) * n_cond + (x % 2) * 2 + core

    places = [
        (y, z, x, core)
        for y in range(n_state)
        for z in range(n_aux // 2)
        for x in range(4)
        for core in range(2)
    ]
    return [(number(*place), number(*step(*place))) for place in places]


def solution(mesh):
    to_core = moves(mesh, lambda y, z, x, c: (y, z, x, 1 - c))
    to_x = {d: moves(mesh, lambda y, z, x, c, d=d: (y, z, x + d, c)) for d in (1, -1, 2)}
    to_pair = moves(mesh, lambda y, z, x, c: (y, z, x ^ 1, c))
    to_y = {d: moves(mesh, lambda y, z, x, c, d=d: (y + d, z, x, c)) for d in (1, -1, 2)}
    n_z = mesh.shape["aux"] // 2
    along_z = [[2 * z + half for z in range(n_z)] for half in range(2)]
    fours = [[4 * g + t for t in range(4)] for g in range(n_z // 2)]
    along_fours = [[4 * g + t for g in range(n_z // 2)] for t in range(4)]

    def send(value, pairs):
        return lax.ppermute(value, AXES, pairs)

    def per_device(cond_pairs, val_pairs, screened, trials):
        n_p, _, _ = cond_pairs.shape
        half = lax.axis_index("aux") % 2
        x_lo = lax.axis_index("cond") // 2

        slabs = [cond_pairs]
        for d in SHIFTS[1:]:
            slabs.append(send(cond_pairs, to_y[d]))
        far = jnp.stack([send(trials[0], to_x[1]), send(trials[1], to_x[-1])])
        pieces = [trials, send(trials, to_core), far]
        pieces.append(send(far, to_core))

        qb, v1, v2 = val_pairs.shape
        spread = val_pairs.reshape(qb, n_z, v1 // n_z, v2).transpose(1, 0, 2, 3)
        spread = lax.all_to_all(spread, "aux", 0, 0, axis_index_groups=along_z)
        n_q = screened.shape[0]
        q = lax.broadcasted_iota(jnp.int32, (n_q, n_q // 2), 0)
        j = lax.broadcasted_iota(jnp.int32, (n_q, n_q // 2), 1)
        picks = (q == (j // qb) * (2 * qb) + half * qb + j % qb).astype(f32)
        columns = jnp.dot(screened, picks, precision=highest)
        spread = spread.reshape(n_q // 2, v1 // n_z, v2)
        product = jnp.einsum("pq,qrv->prv", columns, spread, precision=highest)
        product = product.reshape(n_z, 2, n_p, v1 // n_z, v2)
        swapped = send(lax.dynamic_index_in_dim(product, 1 - half, 1, keepdims=False), to_x[2])
        block = lax.dynamic_index_in_dim(product, half, 1, keepdims=False) + swapped
        block = lax.all_to_all(block, "aux", 0, 0, axis_index_groups=along_z)
        block = block.transpose(1, 0, 2, 3).reshape(n_p, v1, v2)

        other = send(block, to_pair)
        two = jnp.stack([jnp.where(x_lo == 0, block, other), jnp.where(x_lo == 0, other, block)])
        bands = [two]
        for d in SHIFTS[1:]:
            bands.append(send(two, to_y[d]))
        mates = [send(band, to_core) for band in bands]

        m_pair = mix(slabs, pieces)
        partial = respond(m_pair, bands, mates)

        swap = lambda value, groups: lax.all_to_all(value, "aux", 0, 0, axis_index_groups=groups)
        parts = jnp.sum(swap(partial.reshape(4, -1, partial.shape[2]), fours), axis=0)
        parts = jnp.sum(swap(parts.reshape(n_z // 2, -1, parts.shape[1]), along_fours), axis=0)
        copies = lambda value, count: jnp.broadcast_to(value, (count, *value.shape))
        total = swap(copies(parts, n_z // 2), along_fours).reshape(-1, parts.shape[1])
        total = swap(copies(total, 4), fours)
        return total.reshape(partial.shape)

    in_specs = (P("aux", "cond", "state"), P("aux", "state", "cond"), P(), P("state", "cond", None))
    return jax.shard_map(per_device, mesh=mesh, in_specs=in_specs, out_specs=P("state", "cond", None), check_vma=False)
```

```python
import jax
import jax.numpy as jnp
from jax import lax
from jax.experimental import pallas as pl
from jax.experimental.pallas import tpu as pltpu
from jax.sharding import PartitionSpec as P


AXES = ("state", "aux", "cond")
SHIFTS = (0, 1, -1, 2)
highest = lax.Precision.HIGHEST
f32, bf16 = jnp.float32, jnp.bfloat16


def split(value):
    upper = value.astype(bf16)
    return upper, (value - upper.astype(f32)).astype(bf16)


def dot3(a, b):
    (ah, al), (bh, bl) = a, b
    dot = lambda x, y: jnp.dot(x, y, preferred_element_type=f32)
    return dot(ah, bh) + (dot(ah, bl) + dot(al, bh))


def mix_kernel(*refs):
    slabs, pieces, (m, mh, ml), (b_all, x_all, bh, bl, xh, xl, sems) = refs[:4], refs[4:8], refs[8:11], refs[11:]
    n_p, _, width = slabs[0].shape
    n_n = pieces[0].shape[0]
    s, k = lax.axis_index("state"), lax.axis_index("cond")
    copies = []
    for i, shift in enumerate(SHIFTS):
        start = pl.multiple_of(lax.rem(s + 4 - shift, 4) * width, width)
        copies.append(pltpu.make_async_copy(slabs[i], b_all.at[:, :, pl.ds(start, width)], sems.at[i]))
    for i in range(4):
        copies.append(pltpu.make_async_copy(pieces[i], x_all.at[jnp.bitwise_xor(k, i)], sems.at[4 + i]))
    for copy in copies:
        copy.start()
    for copy in copies[4:]:
        copy.wait()

    @pl.loop(0, 4)
    def _(j):
        for n in range(n_n):
            at = pl.ds(pl.multiple_of(j * width, width), width)
            xh[n, at, :], xl[n, at, :] = split(x_all[j, n])

    for copy in copies[:4]:
        copy.wait()

    @pl.loop(0, n_p)
    def _(p):
        bh[...], bl[...] = split(b_all[p])

        @pl.loop(0, n_n)
        def _(n):
            whole = dot3((bh[...], bl[...]), (xh[n], xl[n]))
            m[n, p] = whole
            mh[n, p], ml[n, p] = split(whole)


def mix(slabs, pieces):
    n_p, rows, width = slabs[0].shape
    n_n, _, cols = pieces[0].shape
    any_spec = pl.BlockSpec(memory_space=pl.ANY)
    vmem = pl.BlockSpec(memory_space=pltpu.VMEM)
    shape = (n_n, n_p, rows, cols)
    half = jax.ShapeDtypeStruct(shape, bf16)
    return pl.pallas_call(
        mix_kernel,
        name="mix",
        out_shape=(jax.ShapeDtypeStruct(shape, f32), half, half),
        in_specs=[any_spec] * 8,
        out_specs=(vmem,) * 3,
        scratch_shapes=[
            pltpu.VMEM((n_p, rows, 4 * width), f32),
            pltpu.VMEM((4, n_n, width, cols), f32),
            pltpu.VMEM((rows, 4 * width), bf16),
            pltpu.VMEM((rows, 4 * width), bf16),
            pltpu.VMEM((n_n, 4 * width, cols), bf16),
            pltpu.VMEM((n_n, 4 * width, cols), bf16),
            pltpu.SemaphoreType.DMA((8,)),
        ],
        compiler_params=pltpu.CompilerParams(vmem_limit_bytes=28 << 20),
        cost_estimate=pl.CostEstimate(
            flops=3 * 2 * n_n * n_p * rows * 4 * width * cols, transcendentals=0, bytes_accessed=1 << 24
        ),
    )(*slabs, *pieces)


def halves_kernel(m, mh, ml):
    @pl.loop(0, m.shape[0])
    def _(n):
        @pl.loop(0, m.shape[1])
        def _(p):
            mh[n, p], ml[n, p] = split(m[n, p])


def halves(m):
    half = jax.ShapeDtypeStruct(m.shape, bf16)
    vmem = pl.BlockSpec(memory_space=pltpu.VMEM)
    return pl.pallas_call(
        halves_kernel,
        name="halves",
        out_shape=(half, half),
        in_specs=[vmem],
        out_specs=(vmem, vmem),
        compiler_params=pltpu.CompilerParams(vmem_limit_bytes=16 << 20),
        cost_estimate=pl.CostEstimate(flops=4 * m.size, transcendentals=0, bytes_accessed=8 * m.size),
    )(m)


def respond_kernel(*refs):
    own, partner, blocks, others, (out, c_all, ch, cl, sems) = refs[:2], refs[2:4], refs[4:8], refs[8:12], refs[12:]
    n_n, n_p, rows, _ = own[0].shape
    _, v1, v2 = blocks[0].shape
    s, k = lax.axis_index("state"), lax.axis_index("cond")
    x_lo, core = lax.div(k, 2), lax.rem(k, 2)
    copies = []
    for i, shift in enumerate(SHIFTS):
        row = pl.multiple_of(lax.rem(s + 4 - shift, 4) * v1, v1)
        for block, at in ((blocks[i], x_lo), (others[i], 1 - x_lo)):
            target = c_all.at[:, pl.ds(row, v1), pl.ds(pl.multiple_of(at * v2, v2), v2)]
            copies.append(pltpu.make_async_copy(block, target, sems.at[len(copies)]))
    for copy in copies:
        copy.start()
    out[...] = jnp.zeros_like(out)
    for copy in copies:
        copy.wait()

    @pl.loop(0, n_p)
    def _(p):
        ch[...], cl[...] = split(c_all[p])

        @pl.loop(0, n_n)
        def _(n):
            for (mh, ml), at in ((own, core), (partner, 1 - core)):
                part = dot3((mh[n, p], ml[n, p]), (ch[...], cl[...]))
                for h in range(2):
                    out[2 * n + h, at] += part[h * (rows // 2) : (h + 1) * (rows // 2)]


def respond(own, partner, blocks, others):
    n_n, n_p, rows, cols = own[0].shape
    any_spec = pl.BlockSpec(memory_space=pl.ANY)
    vmem = pl.BlockSpec(memory_space=pltpu.VMEM)
    wide = 2 * blocks[0].shape[2]
    return pl.pallas_call(
        respond_kernel,
        name="respond",
        out_shape=jax.ShapeDtypeStruct((2 * n_n, 2, rows // 2, wide), f32),
        in_specs=[vmem] * 4 + [any_spec] * 8,
        out_specs=vmem,
        scratch_shapes=[
            pltpu.VMEM((n_p, cols, wide), f32),
            pltpu.VMEM((cols, wide), bf16),
            pltpu.VMEM((cols, wide), bf16),
            pltpu.SemaphoreType.DMA((8,)),
        ],
        compiler_params=pltpu.CompilerParams(vmem_limit_bytes=24 << 20),
        cost_estimate=pl.CostEstimate(
            flops=3 * 2 * n_n * n_p * rows * cols * cols, transcendentals=0, bytes_accessed=1 << 24
        ),
    )(*own, *partner, *blocks, *others)


def join_kernel(parts, out, sems):
    copies = []
    for i in range(parts.shape[0]):
        t, core = divmod(i, 2)
        for x in range(2):
            v2 = parts.shape[2] // 2
            source = parts.at[i, :, pl.ds(x * v2, v2)]
            target = out.at[t, :, pl.ds((2 * x + core) * v2, v2)]
            copies.append(pltpu.make_async_copy(source, target, sems.at[len(copies)]))
    for copy in copies:
        copy.start()
    for copy in copies:
        copy.wait()


def join(parts):
    n, rows, cols = parts.shape
    any_spec = pl.BlockSpec(memory_space=pl.ANY)
    return pl.pallas_call(
        join_kernel,
        name="join",
        out_shape=jax.ShapeDtypeStruct((n // 2, rows, 2 * cols), f32),
        in_specs=[any_spec],
        out_specs=any_spec,
        scratch_shapes=[pltpu.SemaphoreType.DMA((2 * n,))],
        compiler_params=pltpu.CompilerParams(vmem_limit_bytes=1 << 20),
        cost_estimate=pl.CostEstimate(flops=0, transcendentals=0, bytes_accessed=8 * parts.size),
    )(parts)


def moves(mesh, step):
    n_state, n_aux, n_cond = (mesh.shape[name] for name in AXES)

    def number(y, z, x, core):
        n_z = n_aux // 2
        y, z, x, core = y % n_state, z % n_z, x % 4, core % 2
        return (y * n_aux + z * 2 + x // 2) * n_cond + (x % 2) * 2 + core

    places = [
        (y, z, x, core)
        for y in range(n_state)
        for z in range(n_aux // 2)
        for x in range(4)
        for core in range(2)
    ]
    return [(number(*place), number(*step(*place))) for place in places]


def solution(mesh):
    to_core = moves(mesh, lambda y, z, x, c: (y, z, x, 1 - c))
    to_x = {d: moves(mesh, lambda y, z, x, c, d=d: (y, z, x + d, c)) for d in (1, -1, 2)}
    to_pair = moves(mesh, lambda y, z, x, c: (y, z, x ^ 1, c))
    to_y = {d: moves(mesh, lambda y, z, x, c, d=d: (y + d, z, x, c)) for d in (1, -1, 2)}
    n_z = mesh.shape["aux"] // 2
    along_z = [[2 * z + half for z in range(n_z)] for half in range(2)]
    fours = [[4 * g + t for t in range(4)] for g in range(n_z // 2)]
    eights = [
        [(4 * g + t) * 4 + 2 * x + core for t in range(4) for core in range(2)] for g in range(n_z // 2) for x in range(2)
    ]
    along_fours = [[4 * g + t for g in range(n_z // 2)] for t in range(4)]

    def send(value, pairs):
        return lax.ppermute(value, AXES, pairs)

    def per_device(cond_pairs, val_pairs, screened, trials):
        n_p, _, _ = cond_pairs.shape
        half = lax.axis_index("aux") % 2

        slabs = [cond_pairs]
        for d in SHIFTS[1:]:
            slabs.append(send(cond_pairs, to_y[d]))
        far = jnp.stack([send(trials[0], to_x[1]), send(trials[1], to_x[-1])])
        pieces = [trials, send(trials, to_core), far]
        pieces.append(send(far, to_core))

        qb, v1, v2 = val_pairs.shape
        spread = val_pairs.reshape(qb, n_z, v1 // n_z, v2).transpose(1, 0, 2, 3)
        spread = lax.all_to_all(spread, "aux", 0, 0, axis_index_groups=along_z)
        n_q = screened.shape[0]
        q = lax.broadcasted_iota(jnp.int32, (n_q, n_q // 2), 0)
        j = lax.broadcasted_iota(jnp.int32, (n_q, n_q // 2), 1)
        picks = (q == (j // qb) * (2 * qb) + half * qb + j % qb).astype(f32)
        columns = jnp.dot(screened, picks, precision=highest)
        spread = spread.reshape(n_q // 2, v1 // n_z, v2)
        product = jnp.einsum("pq,qrv->prv", columns, spread, precision=highest)
        product = product.reshape(n_z, 2, n_p, v1 // n_z, v2)
        swapped = send(lax.dynamic_index_in_dim(product, 1 - half, 1, keepdims=False), to_x[2])
        block = lax.dynamic_index_in_dim(product, half, 1, keepdims=False) + swapped
        block = lax.all_to_all(block, "aux", 0, 0, axis_index_groups=along_z)
        block = block.transpose(1, 0, 2, 3).reshape(n_p, v1, v2)

        mixed, *own = mix(slabs, pieces)
        mixed = send(mixed, to_core)

        other = send(block, to_pair)
        blocks, others = [block], [other]
        for d in SHIFTS[1:]:
            blocks.append(send(block, to_y[d]))
        for d in SHIFTS[1:]:
            others.append(send(other, to_y[d]))
        partner = halves(mixed)
        partial = respond(own, partner, blocks, others)

        def swap(value, groups, axes="aux"):
            return lax.all_to_all(value, axes, 0, 0, axis_index_groups=groups)

        copies = lambda value, count: jnp.broadcast_to(value, (count, *value.shape))
        _, _, part_rows, cols = partial.shape
        parts = jnp.sum(swap(partial.reshape(4, -1, cols), fours), axis=0)
        parts = jnp.sum(swap(parts.reshape(n_z // 2, -1, cols), along_fours), axis=0)
        total = swap(copies(parts, n_z // 2), along_fours).reshape(2, part_rows, cols)
        total = swap(copies(total, 4).reshape(8, part_rows, cols), eights, ("aux", "cond"))
        return join(total).reshape(trials.shape)

    in_specs = (P("aux", "cond", "state"), P("aux", "state", "cond"), P(), P("state", "cond", None))
    return jax.shard_map(per_device, mesh=mesh, in_specs=in_specs, out_specs=P("state", "cond", None), check_vma=False)
```

```python
import jax
import jax.numpy as jnp
from jax import lax
from jax.experimental import pallas as pl
from jax.experimental.pallas import tpu as pltpu
from jax.sharding import PartitionSpec as P


AXES = ("state", "aux", "cond")
SHIFTS = (0, 1, -1, 2)
highest = lax.Precision.HIGHEST
f32, bf16 = jnp.float32, jnp.bfloat16


def split(value):
    upper = value.astype(bf16)
    return upper, (value - upper.astype(f32)).astype(bf16)


def dot3(a, b):
    (ah, al), (bh, bl) = a, b
    dot = lambda x, y: jnp.dot(x, y, preferred_element_type=f32)
    return dot(ah, bh) + (dot(ah, bl) + dot(al, bh))


def mix_kernel(*refs):
    slabs, pieces, (mh, ml), (b_all, x_all, bh, bl, xh, xl, sems) = refs[:4], refs[4:8], refs[8:10], refs[10:]
    n_p, _, width = slabs[0].shape
    n_n = pieces[0].shape[0]
    s, k = lax.axis_index("state"), lax.axis_index("cond")
    copies = []
    for i, shift in enumerate(SHIFTS):
        start = pl.multiple_of(lax.rem(s + 4 - shift, 4) * width, width)
        copies.append(pltpu.make_async_copy(slabs[i], b_all.at[:, :, pl.ds(start, width)], sems.at[i]))
    for i in range(4):
        copies.append(pltpu.make_async_copy(pieces[i], x_all.at[jnp.bitwise_xor(k, i)], sems.at[4 + i]))
    for copy in copies:
        copy.start()
    for copy in copies[4:]:
        copy.wait()

    @pl.loop(0, 4)
    def _(j):
        for n in range(n_n):
            at = pl.ds(pl.multiple_of(j * width, width), width)
            xh[n, at, :], xl[n, at, :] = split(x_all[j, n])

    for copy in copies[:4]:
        copy.wait()

    @pl.loop(0, n_p)
    def _(p):
        bh[...], bl[...] = split(b_all[p])

        @pl.loop(0, n_n)
        def _(n):
            mh[n, p], ml[n, p] = split(dot3((bh[...], bl[...]), (xh[n], xl[n])))


def mix(slabs, pieces):
    n_p, rows, width = slabs[0].shape
    n_n, _, cols = pieces[0].shape
    any_spec = pl.BlockSpec(memory_space=pl.ANY)
    vmem = pl.BlockSpec(memory_space=pltpu.VMEM)
    shape = jax.ShapeDtypeStruct((n_n, n_p, rows, cols), bf16)
    return pl.pallas_call(
        mix_kernel,
        name="mix",
        out_shape=(shape, shape),
        in_specs=[any_spec] * 8,
        out_specs=(vmem, vmem),
        scratch_shapes=[
            pltpu.VMEM((n_p, rows, 4 * width), f32),
            pltpu.VMEM((4, n_n, width, cols), f32),
            pltpu.VMEM((rows, 4 * width), bf16),
            pltpu.VMEM((rows, 4 * width), bf16),
            pltpu.VMEM((n_n, 4 * width, cols), bf16),
            pltpu.VMEM((n_n, 4 * width, cols), bf16),
            pltpu.SemaphoreType.DMA((8,)),
        ],
        compiler_params=pltpu.CompilerParams(vmem_limit_bytes=28 << 20),
        cost_estimate=pl.CostEstimate(
            flops=3 * 2 * n_n * n_p * rows * 4 * width * cols, transcendentals=0, bytes_accessed=1 << 24
        ),
    )(*slabs, *pieces)


def rows_of(m, t, p):
    rows = m.shape[2] // 2
    return m[lax.div(t, 2), p, pl.ds(pl.multiple_of(lax.rem(t, 2) * rows, rows), rows), :]


def add_products(outs, places, mh, ml, p, c_pair):
    both = [jnp.concatenate([rows_of(m, t, p) for t in places], axis=0) for m in (mh, ml)]
    part = dot3(both, c_pair)
    rows = part.shape[0] // 2
    outs[0][...] += part[:rows]
    outs[1][...] += part[rows:]


def far_kernel(*refs):
    mh, ml, bands, mates, (across, diagonal, ch, cl, c_all, sems) = refs[0], refs[1], refs[2:6], refs[6:10], refs[10:]
    n_x, n_p, v1, v2 = bands[0].shape
    s, core = lax.axis_index("state"), lax.rem(lax.axis_index("cond"), 2)
    place = lax.rem(lax.axis_index("aux"), 4)
    copies = []
    for i, shift in enumerate(SHIFTS):
        row = pl.multiple_of(lax.rem(s + 4 - shift, 4) * v1, v1)
        for x in range(n_x):
            for band, at in ((bands[i], core), (mates[i], 1 - core)):
                col = pl.multiple_of((2 * x + at) * v2, v2)
                target = c_all.at[:, pl.ds(row, v1), pl.ds(col, v2)]
                copies.append(pltpu.make_async_copy(band.at[x], target, sems.at[len(copies)]))
    for copy in copies:
        copy.start()
    across[...] = jnp.zeros_like(across)
    diagonal[...] = jnp.zeros_like(diagonal)
    for copy in copies:
        copy.wait()
    places = [jnp.bitwise_xor(place, 1), jnp.bitwise_xor(place, 3)]

    @pl.loop(0, n_p)
    def _(p):
        ch[p], cl[p] = split(c_all[p])
        add_products((across, diagonal), places, mh, ml, p, (ch[p], cl[p]))


def near_kernel(mh, ml, ch, cl, beside, here):
    place = lax.rem(lax.axis_index("aux"), 4)
    places = [jnp.bitwise_xor(place, 2), place]
    beside[...] = jnp.zeros_like(beside)
    here[...] = jnp.zeros_like(here)

    @pl.loop(0, mh.shape[1])
    def _(p):
        add_products((beside, here), places, mh, ml, p, (ch[p], cl[p]))


def respond_far(m_pair, bands, mates):
    _, n_p, rows, cols = m_pair[0].shape
    any_spec = pl.BlockSpec(memory_space=pl.ANY)
    vmem = pl.BlockSpec(memory_space=pltpu.VMEM)
    part = jax.ShapeDtypeStruct((rows // 2, cols), f32)
    full = jax.ShapeDtypeStruct((n_p, cols, cols), bf16)
    return pl.pallas_call(
        far_kernel,
        name="respond_far",
        out_shape=(part, part, full, full),
        in_specs=[vmem] * 2 + [any_spec] * 8,
        out_specs=(vmem,) * 4,
        scratch_shapes=[pltpu.VMEM((n_p, cols, cols), f32), pltpu.SemaphoreType.DMA((16,))],
        compiler_params=pltpu.CompilerParams(vmem_limit_bytes=28 << 20),
        cost_estimate=pl.CostEstimate(flops=6 * n_p * rows * cols * cols, transcendentals=0, bytes_accessed=1 << 23),
    )(*m_pair, *bands, *mates)


def respond_near(m_pair, c_pair):
    _, n_p, rows, cols = m_pair[0].shape
    vmem = pl.BlockSpec(memory_space=pltpu.VMEM)
    part = jax.ShapeDtypeStruct((rows // 2, cols), f32)
    return pl.pallas_call(
        near_kernel,
        name="respond_near",
        out_shape=(part, part),
        in_specs=[vmem] * 4,
        out_specs=(vmem, vmem),
        compiler_params=pltpu.CompilerParams(vmem_limit_bytes=28 << 20),
        cost_estimate=pl.CostEstimate(flops=6 * n_p * rows * cols * cols, transcendentals=0, bytes_accessed=1 << 23),
    )(*m_pair, *c_pair)


def moves(mesh, step):
    n_state, n_aux, n_cond = (mesh.shape[name] for name in AXES)

    def number(y, z, x, core):
        n_z = n_aux // 2
        y, z, x, core = y % n_state, z % n_z, x % 4, core % 2
        return (y * n_aux + z * 2 + x // 2) * n_cond + (x % 2) * 2 + core

    places = [
        (y, z, x, core)
        for y in range(n_state)
        for z in range(n_aux // 2)
        for x in range(4)
        for core in range(2)
    ]
    return [(number(*place), number(*step(*place))) for place in places]


def solution(mesh):
    to_core = moves(mesh, lambda y, z, x, c: (y, z, x, 1 - c))
    to_x = {d: moves(mesh, lambda y, z, x, c, d=d: (y, z, x + d, c)) for d in (1, -1, 2)}
    to_beside = moves(mesh, lambda y, z, x, c: (y, z ^ 1, x, c))
    to_diagonal = moves(mesh, lambda y, z, x, c: (y, z ^ 1, x + 2, c))
    to_pair = moves(mesh, lambda y, z, x, c: (y, z, x ^ 1, c))
    to_y = {d: moves(mesh, lambda y, z, x, c, d=d: (y + d, z, x, c)) for d in (1, -1, 2)}
    n_z = mesh.shape["aux"] // 2
    along_z = [[2 * z + half for z in range(n_z)] for half in range(2)]
    fours = [[4 * g + t for t in range(4)] for g in range(n_z // 2)]
    along_fours = [[4 * g + t for g in range(n_z // 2)] for t in range(4)]

    def send(value, pairs):
        return lax.ppermute(value, AXES, pairs)

    def per_device(cond_pairs, val_pairs, screened, trials):
        n_p, _, _ = cond_pairs.shape
        half = lax.axis_index("aux") % 2
        x_lo = lax.axis_index("cond") // 2

        slabs = [cond_pairs]
        for d in SHIFTS[1:]:
            slabs.append(send(cond_pairs, to_y[d]))
        far = jnp.stack([send(trials[0], to_x[1]), send(trials[1], to_x[-1])])
        pieces = [trials, send(trials, to_core), far]
        pieces.append(send(far, to_core))

        qb, v1, v2 = val_pairs.shape
        spread = val_pairs.reshape(qb, n_z, v1 // n_z, v2).transpose(1, 0, 2, 3)
        spread = lax.all_to_all(spread, "aux", 0, 0, axis_index_groups=along_z)
        n_q = screened.shape[0]
        q = lax.broadcasted_iota(jnp.int32, (n_q, n_q // 2), 0)
        j = lax.broadcasted_iota(jnp.int32, (n_q, n_q // 2), 1)
        picks = (q == (j // qb) * (2 * qb) + half * qb + j % qb).astype(f32)
        columns = jnp.dot(screened, picks, precision=highest)
        spread = spread.reshape(n_q // 2, v1 // n_z, v2)
        product = jnp.einsum("pq,qrv->prv", columns, spread, precision=highest)
        product = product.reshape(n_z, 2, n_p, v1 // n_z, v2)
        swapped = send(lax.dynamic_index_in_dim(product, 1 - half, 1, keepdims=False), to_x[2])
        block = lax.dynamic_index_in_dim(product, half, 1, keepdims=False) + swapped
        block = lax.all_to_all(block, "aux", 0, 0, axis_index_groups=along_z)
        block = block.transpose(1, 0, 2, 3).reshape(n_p, v1, v2)

        other = send(block, to_pair)
        two = jnp.stack([jnp.where(x_lo == 0, block, other), jnp.where(x_lo == 0, other, block)])
        bands = [two]
        for d in SHIFTS[1:]:
            bands.append(send(two, to_y[d]))
        mates = [send(band, to_core) for band in bands]

        m_pair = mix(slabs, pieces)
        across, diagonal, *c_pair = respond_far(m_pair, bands, mates)

        across = send(across, to_x[2])
        diagonal = send(diagonal, to_diagonal)
        beside, here = respond_near(m_pair, c_pair)
        beside = send(beside, to_beside)
        parts = (here + beside) + (across + diagonal)
        swap = lambda value, groups: lax.all_to_all(value, "aux", 0, 0, axis_index_groups=groups)
        parts = jnp.sum(swap(parts.reshape(n_z // 2, -1, parts.shape[1]), along_fours), axis=0)
        copies = lambda value, count: jnp.broadcast_to(value, (count, *value.shape))
        total = swap(copies(parts, n_z // 2), along_fours).reshape(-1, parts.shape[1])
        total = swap(copies(total, 4), fours)
        return total.reshape(trials.shape)

    in_specs = (P("aux", "cond", "state"), P("aux", "state", "cond"), P(), P("state", "cond", None))
    return jax.shard_map(per_device, mesh=mesh, in_specs=in_specs, out_specs=P("state", "cond", None), check_vma=False)
```

```python
import functools

import jax
import jax.numpy as jnp
from jax import lax
from jax.experimental import pallas as pl
from jax.experimental.pallas import tpu as pltpu
from jax.sharding import PartitionSpec as P


AXES = ("state", "aux", "cond")
SHIFTS = (0, 1, -1, 2)
highest = lax.Precision.HIGHEST
f32, bf16 = jnp.float32, jnp.bfloat16


def split(value):
    upper = value.astype(bf16)
    return upper, (value - upper.astype(f32)).astype(bf16)


def dot3(a, b):
    (ah, al), (bh, bl) = a, b
    dot = lambda x, y: jnp.dot(x, y, preferred_element_type=f32)
    return dot(ah, bh) + (dot(ah, bl) + dot(al, bh))


any_spec = pl.BlockSpec(memory_space=pl.ANY)
vmem = pl.BlockSpec(memory_space=pltpu.VMEM)
hbm = pl.BlockSpec(memory_space=pltpu.HBM)


def cost(flops, size):
    return pl.CostEstimate(flops=flops, transcendentals=0, bytes_accessed=size)


def mix_trial(n, pieces, x_all, xh, xl, sems):
    k = lax.axis_index("cond")
    copies = []
    for i in range(4):
        copies.append(pltpu.make_async_copy(pieces[i].at[n], x_all.at[jnp.bitwise_xor(k, i)], sems.at[i]))
    for copy in copies:
        copy.start()
    for copy in copies:
        copy.wait()
    width = x_all.shape[1]

    @pl.loop(0, 4)
    def _(j):
        at = pl.ds(pl.multiple_of(j * width, width), width)
        xh[at, :], xl[at, :] = split(x_all[j])


def mix_first_kernel(*refs):
    slabs, pieces, (m, mh, ml, bh, bl), (b_all, x_all, xh, xl, sems) = refs[:4], refs[4:8], refs[8:13], refs[13:]
    width = slabs[0].shape[2]
    s = lax.axis_index("state")
    copies = []
    for i, shift in enumerate(SHIFTS):
        start = pl.multiple_of(lax.rem(s + 4 - shift, 4) * width, width)
        copies.append(pltpu.make_async_copy(slabs[i], b_all.at[:, :, pl.ds(start, width)], sems.at[4 + i]))
    for copy in copies:
        copy.start()
    mix_trial(0, pieces, x_all, xh, xl, sems)
    for copy in copies:
        copy.wait()

    @pl.loop(0, m.shape[0])
    def _(p):
        bh[p], bl[p] = split(b_all[p])
        whole = dot3((bh[p], bl[p]), (xh[...], xl[...]))
        m[p] = whole
        mh[p], ml[p] = split(whole)


def mix_next_kernel(n, bh, bl, *refs):
    pieces, (m, mh, ml), (x_all, xh, xl, sems) = refs[:4], refs[4:7], refs[7:]
    mix_trial(n, pieces, x_all, xh, xl, sems)

    @pl.loop(0, m.shape[0])
    def _(p):
        whole = dot3((bh[p], bl[p]), (xh[...], xl[...]))
        m[p] = whole
        mh[p], ml[p] = split(whole)


def mix(n, slabs, pieces, b_pair):
    n_p, rows, width = slabs[0].shape
    cols = pieces[0].shape[2]
    shape = (n_p, rows, cols)
    out = [jax.ShapeDtypeStruct(shape, f32)] + [jax.ShapeDtypeStruct(shape, bf16)] * 2
    scratch = [pltpu.VMEM((4, width, cols), f32)] + [pltpu.VMEM((4 * width, cols), bf16)] * 2
    scratch.append(pltpu.SemaphoreType.DMA((8,)))
    kernel, first, specs = functools.partial(mix_next_kernel, n), b_pair, [vmem] * 2
    if b_pair is None:
        kernel, first, specs = mix_first_kernel, slabs, [any_spec] * 4
        out += [jax.ShapeDtypeStruct((n_p, rows, 4 * width), bf16)] * 2
        scratch = [pltpu.VMEM((n_p, rows, 4 * width), f32)] + scratch
    return pl.pallas_call(
        kernel,
        out_shape=tuple(out),
        in_specs=specs + [any_spec] * 4,
        out_specs=(vmem,) * len(out),
        scratch_shapes=scratch,
        compiler_params=pltpu.CompilerParams(vmem_limit_bytes=22 << 20),
        cost_estimate=cost(6 * n_p * rows * 4 * width * cols, 1 << 23),
    )(*first, *pieces)


def halves_kernel(m, mh, ml):
    @pl.loop(0, m.shape[0])
    def _(p):
        mh[p], ml[p] = split(m[p])


def halves(m):
    half = jax.ShapeDtypeStruct(m.shape, bf16)
    return pl.pallas_call(
        halves_kernel,
        name="halves",
        out_shape=(half, half),
        in_specs=[vmem],
        out_specs=(vmem, vmem),
        compiler_params=pltpu.CompilerParams(vmem_limit_bytes=8 << 20),
        cost_estimate=cost(4 * m.size, 8 * m.size),
    )(m)


def bring(sides, h, held, sems):
    rows = held.shape[2]
    at = pl.ds(pl.multiple_of(h * rows, rows), rows)
    copies = [pltpu.make_async_copy(side.at[:, at, :], held.at[i], sems.at[i]) for i, side in enumerate(sides)]
    for copy in copies:
        copy.start()
    return copies


def products(held, p, c_pair):
    upper = jnp.concatenate([held[i, p] for i in range(0, 8, 2)], axis=0)
    lower = jnp.concatenate([held[i, p] for i in range(1, 8, 2)], axis=0)
    return dot3((upper, lower), c_pair)


def deal(total, outs):
    core, place = lax.rem(lax.axis_index("cond"), 2), lax.rem(lax.axis_index("aux"), 4)
    rows = total.shape[0] // 4
    for i, out in enumerate(outs):
        n = jnp.bitwise_xor(lax.div(place, 2), i)
        for side, at in ((0, core), (1, 1 - core)):
            out[at] = total[pl.ds(pl.multiple_of((2 * n + side) * rows, rows), rows), :]


def far_kernel(*refs):
    sides, got, (across, diagonal, ch, cl), (held, c_all, total, sems) = refs[:8], refs[8], refs[9:13], refs[13:]
    _, _, v1, v2 = got.shape
    copies = []
    for i in range(8):
        row, x = divmod(i, 2)
        target = c_all.at[:, pl.ds(row * v1, v1), pl.ds(x * v2, v2)]
        copies.append(pltpu.make_async_copy(got.at[i], target, sems.at[8 + i]))
    for copy in copies:
        copy.start()
    copies += bring(sides, 1 - lax.rem(lax.axis_index("aux"), 2), held, sems)
    total[...] = jnp.zeros_like(total)
    for copy in copies:
        copy.wait()

    @pl.loop(0, c_all.shape[0])
    def _(p):
        ch[p], cl[p] = split(c_all[p])
        total[...] += products(held, p, (ch[p], cl[p]))

    deal(total, (across, diagonal))


def near_kernel(*refs):
    sides, ch, cl, outs, (held, total, sems) = refs[:8], refs[8], refs[9], refs[10:12], refs[12:]
    copies = bring(sides, lax.rem(lax.axis_index("aux"), 2), held, sems)
    total[...] = jnp.zeros_like(total)
    for copy in copies:
        copy.wait()

    @pl.loop(0, ch.shape[0])
    def _(p):
        total[...] += products(held, p, (ch[p], cl[p]))

    deal(total, outs)


def respond_far(sides, got):
    n_p, rows, cols = sides[0].shape
    wide = 2 * got.shape[3]
    part = jax.ShapeDtypeStruct((2, rows // 2, wide), f32)
    full = jax.ShapeDtypeStruct((n_p, cols, wide), bf16)
    return pl.pallas_call(
        far_kernel,
        name="respond_far",
        out_shape=(part, part, full, full),
        in_specs=[hbm] * 8 + [any_spec],
        out_specs=(vmem,) * 4,
        scratch_shapes=[
            pltpu.VMEM((8, n_p, rows // 2, cols), bf16),
            pltpu.VMEM((n_p, cols, wide), f32),
            pltpu.VMEM((2 * rows, wide), f32),
            pltpu.SemaphoreType.DMA((16,)),
        ],
        compiler_params=pltpu.CompilerParams(vmem_limit_bytes=18 << 20),
        cost_estimate=cost(6 * n_p * rows * cols * cols, 1 << 23),
    )(*sides, got)


def respond_near(sides, c_pair):
    n_p, rows, cols = sides[0].shape
    wide = c_pair[0].shape[2]
    part = jax.ShapeDtypeStruct((2, rows // 2, wide), f32)
    return pl.pallas_call(
        near_kernel,
        name="respond_near",
        out_shape=(part, part),
        in_specs=[hbm] * 8 + [vmem] * 2,
        out_specs=(vmem, vmem),
        scratch_shapes=[
            pltpu.VMEM((8, n_p, rows // 2, cols), bf16),
            pltpu.VMEM((2 * rows, wide), f32),
            pltpu.SemaphoreType.DMA((8,)),
        ],
        compiler_params=pltpu.CompilerParams(vmem_limit_bytes=18 << 20),
        cost_estimate=cost(6 * n_p * rows * cols * cols, 1 << 23),
    )(*sides, *c_pair)


def join_kernel(parts, out, sems):
    copies = []
    for i in range(parts.shape[0]):
        t, core = divmod(i, 2)
        for x in range(2):
            v2 = parts.shape[2] // 2
            source = parts.at[i, :, pl.ds(x * v2, v2)]
            target = out.at[t, :, pl.ds((2 * x + core) * v2, v2)]
            copies.append(pltpu.make_async_copy(source, target, sems.at[len(copies)]))
    for copy in copies:
        copy.start()
    for copy in copies:
        copy.wait()


def join(parts):
    n, rows, cols = parts.shape
    return pl.pallas_call(
        join_kernel,
        name="join",
        out_shape=jax.ShapeDtypeStruct((n // 2, rows, 2 * cols), f32),
        in_specs=[any_spec],
        out_specs=any_spec,
        scratch_shapes=[pltpu.SemaphoreType.DMA((2 * n,))],
        compiler_params=pltpu.CompilerParams(vmem_limit_bytes=1 << 20),
        cost_estimate=cost(0, 8 * parts.size),
    )(parts)


def moves(mesh, step):
    n_state, n_aux, n_cond = (mesh.shape[name] for name in AXES)

    def number(y, z, x, core):
        n_z = n_aux // 2
        y, z, x, core = y % n_state, z % n_z, x % 4, core % 2
        return (y * n_aux + z * 2 + x // 2) * n_cond + (x % 2) * 2 + core

    places = [
        (y, z, x, core)
        for y in range(n_state)
        for z in range(n_aux // 2)
        for x in range(4)
        for core in range(2)
    ]
    return [(number(*place), number(*step(*place))) for place in places]


def solution(mesh):
    to_core = moves(mesh, lambda y, z, x, c: (y, z, x, 1 - c))
    to_x = {d: moves(mesh, lambda y, z, x, c, d=d: (y, z, x + d, c)) for d in (1, -1, 2)}
    to_beside = moves(mesh, lambda y, z, x, c: (y, z ^ 1, x, c))
    to_diagonal = moves(mesh, lambda y, z, x, c: (y, z ^ 1, x + 2, c))
    to_y = {d: moves(mesh, lambda y, z, x, c, d=d: (y + d, z, x, c)) for d in (1, -1, 2)}
    n_z = mesh.shape["aux"] // 2
    along_z = [[2 * z + half for z in range(n_z)] for half in range(2)]
    eights = [
        [(4 * g + t) * 4 + 2 * x + core for t in range(4) for core in range(2)] for g in range(n_z // 2) for x in range(2)
    ]
    sheets = [[4 * s + 2 * x + core for s in range(4) for x in range(2)] for core in range(2)]
    along_fours = [[4 * g + t for g in range(n_z // 2)] for t in range(4)]

    def send(value, pairs):
        return lax.ppermute(value, AXES, pairs)

    def per_device(cond_pairs, val_pairs, screened, trials):
        n_p, _, _ = cond_pairs.shape
        half = lax.axis_index("aux") % 2

        slabs = [cond_pairs]
        for d in SHIFTS[1:]:
            slabs.append(send(cond_pairs, to_y[d]))
        far = jnp.stack([send(trials[0], to_x[1]), send(trials[1], to_x[-1])])
        pieces = [trials, send(trials, to_core), far]
        pieces.append(send(far, to_core))

        qb, v1, v2 = val_pairs.shape
        spread = val_pairs.reshape(qb, n_z, v1 // n_z, v2).transpose(1, 0, 2, 3)
        spread = lax.all_to_all(spread, "aux", 0, 0, axis_index_groups=along_z)
        n_q = screened.shape[0]
        q = lax.broadcasted_iota(jnp.int32, (n_q, n_q // 2), 0)
        j = lax.broadcasted_iota(jnp.int32, (n_q, n_q // 2), 1)
        picks = (q == (j // qb) * (2 * qb) + half * qb + j % qb).astype(f32)
        columns = jnp.dot(screened, picks, precision=highest)
        spread = spread.reshape(n_q // 2, v1 // n_z, v2)
        product = jnp.einsum("pq,qrv->prv", columns, spread, precision=highest)
        product = product.reshape(n_z, 2, n_p, v1 // n_z, v2)
        swapped = send(lax.dynamic_index_in_dim(product, 1 - half, 1, keepdims=False), to_x[2])
        block = lax.dynamic_index_in_dim(product, half, 1, keepdims=False) + swapped
        block = lax.all_to_all(block, "aux", 0, 0, axis_index_groups=along_z)
        block = block.transpose(1, 0, 2, 3).reshape(n_p, v1, v2)

        copies = lambda value, count: jnp.broadcast_to(value, (count, *value.shape))
        swap = lambda value, groups, axes="aux": lax.all_to_all(value, axes, 0, 0, axis_index_groups=groups)

        got = swap(copies(block, 8), sheets, ("state", "cond"))

        own, partner, b_pair = [], [], None
        for n in range(trials.shape[0]):
            mixed, upper, lower, *b_new = mix(n, slabs, pieces, b_pair)
            b_pair = b_pair or b_new
            mixed = send(mixed, to_core)
            own, partner = [*own, (upper, lower)], [*partner, halves(mixed)]
        sides = [part for pair in zip(own, partner) for half_pair in pair for part in half_pair]
        sides = [pltpu.with_memory_space_constraint(side, pltpu.HBM) for side in sides]
        across, diagonal, *c_pair = respond_far(sides, got)

        across = send(across, to_x[2])
        diagonal = send(diagonal, to_diagonal)
        here, beside = respond_near(sides, c_pair)
        beside = send(beside, to_beside)
        parts = (here + beside) + (across + diagonal)
        shape = parts.shape
        parts = jnp.sum(swap(parts.reshape(n_z // 2, -1, shape[2]), along_fours), axis=0)
        total = swap(copies(parts, n_z // 2), along_fours).reshape(shape)
        total = swap(copies(total, 4).reshape(8, *shape[1:]), eights, ("aux", "cond"))
        return join(total).reshape(trials.shape)

    in_specs = (P("aux", "cond", "state"), P("aux", "state", "cond"), P(), P("state", "cond", None))
    return jax.shard_map(per_device, mesh=mesh, in_specs=in_specs, out_specs=P("state", "cond", None), check_vma=False)
```

```python
import jax
import jax.numpy as jnp
from jax import lax
from jax.experimental import pallas as pl
from jax.experimental.pallas import tpu as pltpu
from jax.sharding import PartitionSpec as P


AXES = ("state", "aux", "cond")
SHIFTS = (0, 1, -1, 2)
highest = lax.Precision.HIGHEST
f32, bf16 = jnp.float32, jnp.bfloat16


def split(value):
    upper = value.astype(bf16)
    return upper, (value - upper.astype(f32)).astype(bf16)


def dot3(a, b):
    (ah, al), (bh, bl) = a, b
    dot = lambda x, y: jnp.dot(x, y, preferred_element_type=f32)
    return dot(ah, bh) + (dot(ah, bl) + dot(al, bh))


def mix_kernel(*refs):
    slabs, pieces, (mh, ml), (b_all, x_all, xh, xl, sems) = refs[:4], refs[4:8], refs[8:10], refs[10:]
    n_p, _, width = slabs[0].shape
    n_n = pieces[0].shape[0]
    s, k = lax.axis_index("state"), lax.axis_index("cond")
    copies = []
    for i, shift in enumerate(SHIFTS):
        start = pl.multiple_of(lax.rem(s + 4 - shift, 4) * width, width)
        copies.append(pltpu.make_async_copy(slabs[i], b_all.at[:, :, pl.ds(start, width)], sems.at[i]))
    for i in range(4):
        copies.append(pltpu.make_async_copy(pieces[i], x_all.at[jnp.bitwise_xor(k, i)], sems.at[4 + i]))
    for copy in copies:
        copy.start()
    for copy in copies[4:]:
        copy.wait()

    @pl.loop(0, 4)
    def _(j):
        for n in range(n_n):
            at = pl.ds(pl.multiple_of(j * width, width), width)
            xh[n, at, :], xl[n, at, :] = split(x_all[j, n])

    for copy in copies[:4]:
        copy.wait()

    for p in range(n_p):
        slab = split(b_all[p])
        for n in range(n_n):
            mh[n, p], ml[n, p] = split(dot3(slab, (xh[n], xl[n])))


def mix(slabs, pieces):
    n_p, rows, width = slabs[0].shape
    n_n, _, cols = pieces[0].shape
    any_spec = pl.BlockSpec(memory_space=pl.ANY)
    vmem = pl.BlockSpec(memory_space=pltpu.VMEM)
    shape = jax.ShapeDtypeStruct((n_n, n_p, rows, cols), bf16)
    return pl.pallas_call(
        mix_kernel,
        name="mix",
        out_shape=(shape, shape),
        in_specs=[any_spec] * 8,
        out_specs=(vmem, vmem),
        scratch_shapes=[
            pltpu.VMEM((n_p, rows, 4 * width), f32),
            pltpu.VMEM((4, n_n, width, cols), f32),
            pltpu.VMEM((n_n, 4 * width, cols), bf16),
            pltpu.VMEM((n_n, 4 * width, cols), bf16),
            pltpu.SemaphoreType.DMA((8,)),
        ],
        compiler_params=pltpu.CompilerParams(vmem_limit_bytes=28 << 20),
        cost_estimate=pl.CostEstimate(
            flops=3 * 2 * n_n * n_p * rows * 4 * width * cols, transcendentals=0, bytes_accessed=1 << 24
        ),
    )(*slabs, *pieces)


def rows_of(m, t, p):
    rows = m.shape[2] // 2
    return m[lax.div(t, 2), p, pl.ds(pl.multiple_of(lax.rem(t, 2) * rows, rows), rows), :]


def add_products(outs, places, mh, ml, p, c_pair):
    part = dot3([jnp.concatenate([rows_of(m, t, p) for t in places], axis=0) for m in (mh, ml)], c_pair)
    rows = outs[0].shape[0]
    for i, out in enumerate(outs):
        out[...] += part[i * rows : (i + 1) * rows]


def far_kernel(*refs):
    mh, ml, bands, mates, (*outs, ch, cl, c_all, sems) = refs[0], refs[1], refs[2:6], refs[6:10], refs[10:]
    n_x, n_p, v1, v2 = bands[0].shape
    s, core = lax.axis_index("state"), lax.rem(lax.axis_index("cond"), 2)
    place = lax.rem(lax.axis_index("aux"), 4)
    copies = []
    for i, shift in enumerate(SHIFTS):
        row = pl.multiple_of(lax.rem(s + 4 - shift, 4) * v1, v1)
        for x in range(n_x):
            for band, at in ((bands[i], core), (mates[i], 1 - core)):
                col = pl.multiple_of((2 * x + at) * v2, v2)
                target = c_all.at[:, pl.ds(row, v1), pl.ds(col, v2)]
                copies.append(pltpu.make_async_copy(band.at[x], target, sems.at[len(copies)]))
    for copy in copies:
        copy.start()
    for out in outs:
        out[...] = jnp.zeros_like(out)
    for copy in copies:
        copy.wait()
    places = [jnp.bitwise_xor(place, t) for t in (1, 3, 2)]

    @pl.loop(0, n_p)
    def _(p):
        ch[p], cl[p] = split(c_all[p])
        add_products(outs, places, mh, ml, p, (ch[p], cl[p]))


def near_kernel(mh, ml, ch, cl, here):
    place = lax.rem(lax.axis_index("aux"), 4)
    here[...] = jnp.zeros_like(here)

    @pl.loop(0, mh.shape[1])
    def _(p):
        add_products((here,), (place,), mh, ml, p, (ch[p], cl[p]))


def respond_far(m_pair, bands, mates):
    _, n_p, rows, cols = m_pair[0].shape
    any_spec = pl.BlockSpec(memory_space=pl.ANY)
    vmem = pl.BlockSpec(memory_space=pltpu.VMEM)
    part = jax.ShapeDtypeStruct((rows // 2, cols), f32)
    full = jax.ShapeDtypeStruct((n_p, cols, cols), bf16)
    return pl.pallas_call(
        far_kernel,
        name="respond_far",
        out_shape=(part, part, part, full, full),
        in_specs=[vmem] * 2 + [any_spec] * 8,
        out_specs=(vmem,) * 5,
        scratch_shapes=[pltpu.VMEM((n_p, cols, cols), f32), pltpu.SemaphoreType.DMA((16,))],
        compiler_params=pltpu.CompilerParams(vmem_limit_bytes=28 << 20),
        cost_estimate=pl.CostEstimate(flops=6 * n_p * rows * cols * cols, transcendentals=0, bytes_accessed=1 << 23),
    )(*m_pair, *bands, *mates)


def respond_near(m_pair, c_pair):
    _, n_p, rows, cols = m_pair[0].shape
    vmem = pl.BlockSpec(memory_space=pltpu.VMEM)
    part = jax.ShapeDtypeStruct((rows // 2, cols), f32)
    return pl.pallas_call(
        near_kernel,
        name="respond_near",
        out_shape=part,
        in_specs=[vmem] * 4,
        out_specs=vmem,
        compiler_params=pltpu.CompilerParams(vmem_limit_bytes=28 << 20),
        cost_estimate=pl.CostEstimate(flops=6 * n_p * rows * cols * cols, transcendentals=0, bytes_accessed=1 << 23),
    )(*m_pair, *c_pair)


def moves(mesh, step):
    n_state, n_aux, n_cond = (mesh.shape[name] for name in AXES)

    def number(y, z, x, core):
        n_z = n_aux // 2
        y, z, x, core = y % n_state, z % n_z, x % 4, core % 2
        return (y * n_aux + z * 2 + x // 2) * n_cond + (x % 2) * 2 + core

    places = [
        (y, z, x, core)
        for y in range(n_state)
        for z in range(n_aux // 2)
        for x in range(4)
        for core in range(2)
    ]
    return [(number(*place), number(*step(*place))) for place in places]


def solution(mesh):
    to_core = moves(mesh, lambda y, z, x, c: (y, z, x, 1 - c))
    to_x = {d: moves(mesh, lambda y, z, x, c, d=d: (y, z, x + d, c)) for d in (1, -1, 2)}
    to_beside = moves(mesh, lambda y, z, x, c: (y, z ^ 1, x, c))
    to_diagonal = moves(mesh, lambda y, z, x, c: (y, z ^ 1, x + 2, c))
    to_pair = moves(mesh, lambda y, z, x, c: (y, z, x ^ 1, c))
    to_y = {d: moves(mesh, lambda y, z, x, c, d=d: (y + d, z, x, c)) for d in (1, -1, 2)}
    n_z = mesh.shape["aux"] // 2
    along_z = [[2 * z + half for z in range(n_z)] for half in range(2)]
    fours = [[4 * g + t for t in range(4)] for g in range(n_z // 2)]
    along_fours = [[4 * g + t for g in range(n_z // 2)] for t in range(4)]

    def send(value, pairs):
        return lax.ppermute(value, AXES, pairs)

    def per_device(cond_pairs, val_pairs, screened, trials):
        n_p, _, _ = cond_pairs.shape
        half = lax.axis_index("aux") % 2
        x_lo = lax.axis_index("cond") // 2

        slabs = [cond_pairs]
        for d in SHIFTS[1:]:
            slabs.append(send(cond_pairs, to_y[d]))
        far = jnp.stack([send(trials[0], to_x[1]), send(trials[1], to_x[-1])])
        pieces = [trials, send(trials, to_core), far]
        pieces.append(send(far, to_core))

        qb, v1, v2 = val_pairs.shape
        spread = val_pairs.reshape(qb, n_z, v1 // n_z, v2).transpose(1, 0, 2, 3)
        spread = lax.all_to_all(spread, "aux", 0, 0, axis_index_groups=along_z)
        n_q = screened.shape[0]
        q = lax.broadcasted_iota(jnp.int32, (n_q, n_q // 2), 0)
        j = lax.broadcasted_iota(jnp.int32, (n_q, n_q // 2), 1)
        picks = (q == (j // qb) * (2 * qb) + half * qb + j % qb).astype(f32)
        columns = jnp.dot(screened, picks, precision=highest)
        spread = spread.reshape(n_q // 2, v1 // n_z, v2)
        product = jnp.einsum("pq,qrv->prv", columns, spread, precision=highest)
        product = product.reshape(n_z, 2, n_p, v1 // n_z, v2)
        swapped = send(lax.dynamic_index_in_dim(product, 1 - half, 1, keepdims=False), to_x[2])
        block = lax.dynamic_index_in_dim(product, half, 1, keepdims=False) + swapped
        block = lax.all_to_all(block, "aux", 0, 0, axis_index_groups=along_z)
        block = block.transpose(1, 0, 2, 3).reshape(n_p, v1, v2)

        other = send(block, to_pair)
        two = jnp.stack([jnp.where(x_lo == 0, block, other), jnp.where(x_lo == 0, other, block)])
        bands = [two]
        for d in SHIFTS[1:]:
            bands.append(send(two, to_y[d]))
        mates = [send(band, to_core) for band in bands]

        m_pair = mix(slabs, pieces)
        across, diagonal, beside, *c_pair = respond_far(m_pair, bands, mates)

        across = send(across, to_x[2])
        diagonal = send(diagonal, to_diagonal)
        beside = send(beside, to_beside)
        here = respond_near(m_pair, c_pair)
        parts = (here + beside) + (across + diagonal)
        swap = lambda value, groups: lax.all_to_all(value, "aux", 0, 0, axis_index_groups=groups)
        parts = jnp.sum(swap(parts.reshape(n_z // 2, -1, parts.shape[1]), along_fours), axis=0)
        copies = lambda value, count: jnp.broadcast_to(value, (count, *value.shape))
        total = swap(copies(parts, n_z // 2), along_fours).reshape(-1, parts.shape[1])
        total = swap(copies(total, 4), fours)
        return total.reshape(trials.shape)

    in_specs = (P("aux", "cond", "state"), P("aux", "state", "cond"), P(), P("state", "cond", None))
    return jax.shard_map(per_device, mesh=mesh, in_specs=in_specs, out_specs=P("state", "cond", None), check_vma=False)
```

```python
import jax
import jax.numpy as jnp
from jax import lax
from jax.experimental import pallas as pl
from jax.experimental.pallas import tpu as pltpu
from jax.sharding import PartitionSpec as P


AXES = ("state", "aux", "cond")
SHIFTS = (0, 1, -1, 2)
highest = lax.Precision.HIGHEST
f32, bf16 = jnp.float32, jnp.bfloat16


def split(value):
    upper = value.astype(bf16)
    return upper, (value - upper.astype(f32)).astype(bf16)


def dot3(a, b):
    (ah, al), (bh, bl) = a, b
    dot = lambda x, y: jnp.dot(x, y, preferred_element_type=f32)
    return dot(ah, bh) + (dot(ah, bl) + dot(al, bh))


def mix_kernel(*refs):
    slabs, pieces, (mh, ml), (b_all, x_all, bh, bl, xh, xl, sems) = refs[:4], refs[4:8], refs[8:10], refs[10:]
    n_p, _, width = slabs[0].shape
    n_n = pieces[0].shape[0]
    s, k = lax.axis_index("state"), lax.axis_index("cond")
    copies = []
    for i, shift in enumerate(SHIFTS):
        start = pl.multiple_of(lax.rem(s + 4 - shift, 4) * width, width)
        copies.append(pltpu.make_async_copy(slabs[i], b_all.at[:, :, pl.ds(start, width)], sems.at[i]))
    for i in range(4):
        copies.append(pltpu.make_async_copy(pieces[i], x_all.at[jnp.bitwise_xor(k, i)], sems.at[4 + i]))
    for copy in copies:
        copy.start()
    for copy in copies[4:]:
        copy.wait()

    @pl.loop(0, 4)
    def _(j):
        for n in range(n_n):
            at = pl.ds(pl.multiple_of(j * width, width), width)
            xh[n, at, :], xl[n, at, :] = split(x_all[j, n])

    for copy in copies[:4]:
        copy.wait()

    @pl.loop(0, n_p)
    def _(p):
        bh[...], bl[...] = split(b_all[p])

        @pl.loop(0, n_n)
        def _(n):
            mh[n, p], ml[n, p] = split(dot3((bh[...], bl[...]), (xh[n], xl[n])))


def mix(slabs, pieces):
    n_p, rows, width = slabs[0].shape
    n_n, _, cols = pieces[0].shape
    any_spec = pl.BlockSpec(memory_space=pl.ANY)
    vmem = pl.BlockSpec(memory_space=pltpu.VMEM)
    shape = jax.ShapeDtypeStruct((n_n, n_p, rows, cols), bf16)
    return pl.pallas_call(
        mix_kernel,
        name="mix",
        out_shape=(shape, shape),
        in_specs=[any_spec] * 8,
        out_specs=(vmem, vmem),
        scratch_shapes=[
            pltpu.VMEM((n_p, rows, 4 * width), f32),
            pltpu.VMEM((4, n_n, width, cols), f32),
            pltpu.VMEM((rows, 4 * width), bf16),
            pltpu.VMEM((rows, 4 * width), bf16),
            pltpu.VMEM((n_n, 4 * width, cols), bf16),
            pltpu.VMEM((n_n, 4 * width, cols), bf16),
            pltpu.SemaphoreType.DMA((8,)),
        ],
        compiler_params=pltpu.CompilerParams(vmem_limit_bytes=28 << 20),
        cost_estimate=pl.CostEstimate(
            flops=3 * 2 * n_n * n_p * rows * 4 * width * cols, transcendentals=0, bytes_accessed=1 << 24
        ),
    )(*slabs, *pieces)


def rows_of(m, t, p):
    rows = m.shape[2] // 2
    return m[lax.div(t, 2), p, pl.ds(pl.multiple_of(lax.rem(t, 2) * rows, rows), rows), :]


def add_products(outs, places, mh, ml, p, c_pair):
    both = [jnp.concatenate([rows_of(m, t, p) for t in places], axis=0) for m in (mh, ml)]
    part = dot3(both, c_pair)
    rows = part.shape[0] // 2
    outs[0][...] += part[:rows]
    outs[1][...] += part[rows:]


def far_kernel(*refs):
    mh, ml, bands, mates, (across, diagonal, ch, cl, c_all, sems) = refs[0], refs[1], refs[2:6], refs[6:10], refs[10:]
    n_x, n_p, v1, v2 = bands[0].shape
    s, core = lax.axis_index("state"), lax.rem(lax.axis_index("cond"), 2)
    place = lax.rem(lax.axis_index("aux"), 4)
    copies = []
    for i, shift in enumerate(SHIFTS):
        row = pl.multiple_of(lax.rem(s + 4 - shift, 4) * v1, v1)
        for x in range(n_x):
            for band, at in ((bands[i], core), (mates[i], 1 - core)):
                col = pl.multiple_of((2 * x + at) * v2, v2)
                target = c_all.at[:, pl.ds(row, v1), pl.ds(col, v2)]
                copies.append(pltpu.make_async_copy(band.at[x], target, sems.at[len(copies)]))
    for copy in copies:
        copy.start()
    across[...] = jnp.zeros_like(across)
    diagonal[...] = jnp.zeros_like(diagonal)
    for copy in copies:
        copy.wait()
    places = [jnp.bitwise_xor(place, 1), jnp.bitwise_xor(place, 3)]

    @pl.loop(0, n_p)
    def _(p):
        ch[p], cl[p] = split(c_all[p])
        add_products((across, diagonal), places, mh, ml, p, (ch[p], cl[p]))


def near_kernel(mh, ml, ch, cl, beside, here):
    place = lax.rem(lax.axis_index("aux"), 4)
    places = [jnp.bitwise_xor(place, 2), place]
    beside[...] = jnp.zeros_like(beside)
    here[...] = jnp.zeros_like(here)

    @pl.loop(0, mh.shape[1])
    def _(p):
        add_products((beside, here), places, mh, ml, p, (ch[p], cl[p]))


def respond_far(m_pair, bands, mates):
    _, n_p, rows, cols = m_pair[0].shape
    any_spec = pl.BlockSpec(memory_space=pl.ANY)
    vmem = pl.BlockSpec(memory_space=pltpu.VMEM)
    part = jax.ShapeDtypeStruct((rows // 2, cols), f32)
    full = jax.ShapeDtypeStruct((n_p, cols, cols), bf16)
    return pl.pallas_call(
        far_kernel,
        name="respond_far",
        out_shape=(part, part, full, full),
        in_specs=[vmem] * 2 + [any_spec] * 8,
        out_specs=(vmem,) * 4,
        scratch_shapes=[pltpu.VMEM((n_p, cols, cols), f32), pltpu.SemaphoreType.DMA((16,))],
        compiler_params=pltpu.CompilerParams(vmem_limit_bytes=28 << 20),
        cost_estimate=pl.CostEstimate(flops=6 * n_p * rows * cols * cols, transcendentals=0, bytes_accessed=1 << 23),
    )(*m_pair, *bands, *mates)


def respond_near(m_pair, c_pair):
    _, n_p, rows, cols = m_pair[0].shape
    vmem = pl.BlockSpec(memory_space=pltpu.VMEM)
    part = jax.ShapeDtypeStruct((rows // 2, cols), f32)
    return pl.pallas_call(
        near_kernel,
        name="respond_near",
        out_shape=(part, part),
        in_specs=[vmem] * 4,
        out_specs=(vmem, vmem),
        compiler_params=pltpu.CompilerParams(vmem_limit_bytes=28 << 20),
        cost_estimate=pl.CostEstimate(flops=6 * n_p * rows * cols * cols, transcendentals=0, bytes_accessed=1 << 23),
    )(*m_pair, *c_pair)


def deal_kernel(blocks, out, sems):
    copies = [pltpu.make_async_copy(blocks.at[q], out.at[:, q], sems.at[q]) for q in range(blocks.shape[0])]
    for copy in copies:
        copy.start()
    for copy in copies:
        copy.wait()


def deal(blocks):
    n_q, n, rows, cols = blocks.shape
    return pl.pallas_call(
        deal_kernel,
        name="deal",
        out_shape=jax.ShapeDtypeStruct((n, n_q, rows, cols), f32),
        in_specs=[pl.BlockSpec(memory_space=pl.ANY)],
        out_specs=pl.BlockSpec(memory_space=pl.ANY),
        scratch_shapes=[pltpu.SemaphoreType.DMA((n_q,))],
        compiler_params=pltpu.CompilerParams(vmem_limit_bytes=2 << 20),
        cost_estimate=pl.CostEstimate(flops=0, transcendentals=0, bytes_accessed=8 * blocks.size),
    )(blocks)


def moves(mesh, step):
    n_state, n_aux, n_cond = (mesh.shape[name] for name in AXES)

    def number(y, z, x, core):
        n_z = n_aux // 2
        y, z, x, core = y % n_state, z % n_z, x % 4, core % 2
        return (y * n_aux + z * 2 + x // 2) * n_cond + (x % 2) * 2 + core

    places = [
        (y, z, x, core)
        for y in range(n_state)
        for z in range(n_aux // 2)
        for x in range(4)
        for core in range(2)
    ]
    return [(number(*place), number(*step(*place))) for place in places]


def solution(mesh):
    to_core = moves(mesh, lambda y, z, x, c: (y, z, x, 1 - c))
    to_x = {d: moves(mesh, lambda y, z, x, c, d=d: (y, z, x + d, c)) for d in (1, -1, 2)}
    to_beside = moves(mesh, lambda y, z, x, c: (y, z ^ 1, x, c))
    to_diagonal = moves(mesh, lambda y, z, x, c: (y, z ^ 1, x + 2, c))
    to_pair = moves(mesh, lambda y, z, x, c: (y, z, x ^ 1, c))
    to_y = {d: moves(mesh, lambda y, z, x, c, d=d: (y + d, z, x, c)) for d in (1, -1, 2)}
    n_z = mesh.shape["aux"] // 2
    along_z = [[2 * z + half for z in range(n_z)] for half in range(2)]
    fours = [[4 * g + t for t in range(4)] for g in range(n_z // 2)]
    along_fours = [[4 * g + t for g in range(n_z // 2)] for t in range(4)]

    def send(value, pairs):
        return lax.ppermute(value, AXES, pairs)

    def per_device(cond_pairs, val_pairs, screened, trials):
        n_p, _, _ = cond_pairs.shape
        half = lax.axis_index("aux") % 2
        x_lo = lax.axis_index("cond") // 2

        slabs = [cond_pairs]
        for d in SHIFTS[1:]:
            slabs.append(send(cond_pairs, to_y[d]))
        far = jnp.stack([send(trials[0], to_x[1]), send(trials[1], to_x[-1])])
        pieces = [trials, send(trials, to_core), far]
        pieces.append(send(far, to_core))

        qb, v1, v2 = val_pairs.shape
        spread = deal(val_pairs.reshape(qb, n_z, v1 // n_z, v2))
        spread = lax.all_to_all(spread, "aux", 0, 0, axis_index_groups=along_z)
        n_q = screened.shape[0]
        q = lax.broadcasted_iota(jnp.int32, (n_q, n_q // 2), 0)
        j = lax.broadcasted_iota(jnp.int32, (n_q, n_q // 2), 1)
        picks = (q == (j // qb) * (2 * qb) + half * qb + j % qb).astype(f32)
        columns = jnp.dot(screened, picks, precision=highest)
        spread = spread.reshape(n_q // 2, v1 // n_z, v2)
        product = jnp.einsum("pq,qrv->prv", columns, spread, precision=highest)
        product = product.reshape(n_z, 2, n_p, v1 // n_z, v2)
        swapped = send(lax.dynamic_index_in_dim(product, 1 - half, 1, keepdims=False), to_x[2])
        block = lax.dynamic_index_in_dim(product, half, 1, keepdims=False) + swapped
        block = lax.all_to_all(block, "aux", 0, 0, axis_index_groups=along_z)
        block = block.transpose(1, 0, 2, 3).reshape(n_p, v1, v2)

        other = send(block, to_pair)
        two = jnp.stack([jnp.where(x_lo == 0, block, other), jnp.where(x_lo == 0, other, block)])
        bands = [two]
        for d in SHIFTS[1:]:
            bands.append(send(two, to_y[d]))
        mates = [send(band, to_core) for band in bands]

        m_pair = mix(slabs, pieces)
        across, diagonal, *c_pair = respond_far(m_pair, bands, mates)

        across = send(across, to_x[2])
        diagonal = send(diagonal, to_diagonal)
        beside, here = respond_near(m_pair, c_pair)
        beside = send(beside, to_beside)
        parts = (here + beside) + (across + diagonal)
        swap = lambda value, groups: lax.all_to_all(value, "aux", 0, 0, axis_index_groups=groups)
        parts = jnp.sum(swap(parts.reshape(n_z // 2, -1, parts.shape[1]), along_fours), axis=0)
        copies = lambda value, count: jnp.broadcast_to(value, (count, *value.shape))
        total = swap(copies(parts, n_z // 2), along_fours).reshape(-1, parts.shape[1])
        total = swap(copies(total, 4), fours)
        return total.reshape(trials.shape)

    in_specs = (P("aux", "cond", "state"), P("aux", "state", "cond"), P(), P("state", "cond", None))
    return jax.shard_map(per_device, mesh=mesh, in_specs=in_specs, out_specs=P("state", "cond", None), check_vma=False)
```
